32 devices in a mesh: ty: 4 (over y, x), tx: 8 (over z, core).
Axes of the slice: x: 2, y: 2, z: 4, core: 2. Of those that a mesh axis runs over, the one named last changes fastest.
Arguments:
- block_sums: float32 [4096, 1, 1024], P(('ty', 'tx')), may hold values from -6 to 6
- block_weights: float32 [4096, 1, 1024], P(('ty', 'tx')), may hold values from 0.1 to 2
- block_tile: int32 [4096, 1], P(('ty', 'tx')), may hold values from 0 to 31; in each aligned block of 128 rows (0 to 127, 128 to 255, ...) at most 8 rows name the same one
- block_row: int32 [4096], P(('ty', 'tx')), may hold values from 0 to 127
- prior_weight: float32 [512, 8192], P('ty', 'tx'), may hold values from 0.1 to 1
Outputs:
- solution_field: float32 [512, 8192], P('ty', 'tx')
- residual: float32 [512, 8192], P('ty', 'tx')
The draws below stay inside these ranges and needn't reach their ends.
Inputs may be any that keep to these rules, and one draw needn't show every extreme that they name: `block_tile`: among the 128 blocks of one log shard no tile is named more than 8 times, a bound that some block reaches.
All inputs are finite; a program needn't handle non-finite values.
Results may differ from the reference program's by a relative error of at most 0.0003.
Values sent between devices are 32-bit elements; how exact they have to be, the bound alone decides.
A program may use at most 64 MiB of HBM per device.

```python
import math
import jax
import jax.numpy as jnp
import numpy as np
from jax import lax

ROWS = 128
COLS = 1024
HALF = 32
ITERS = 2
BLK_DEV = 128
BAND = 1
CAP = 8
BLOCKS = 4096
NY = 512
NX = 8192
N_TX = 8
DEVICES = 32


def set_ends(drawn, rng, least, top_value):
    extent = drawn.shape
    index_at = [jax.random.randint(jax.random.fold_in(rng, axis), (), 0, extent[axis]) for axis in range(len(extent))]
    drawn = drawn.at[tuple(index_at)].set(least)
    longest = extent.index(max(extent))
    index_at[longest] = (index_at[longest] + 1) % extent[longest]
    return drawn.at[tuple(index_at)].set(top_value)


def steps_of(stream_key, shape, cuts, smallest, top_value):
    level = 1.0
    for axis_at, parts in cuts:
        heights = jax.random.uniform(jax.random.fold_in(jax.random.fold_in(stream_key, 6), axis_at), (parts,), jnp.float32, smallest / len(cuts), top_value / len(cuts))
        level = level * jnp.repeat(jnp.exp(heights), shape[axis_at] // parts).reshape((-1,) + (1,) * (len(shape) - 1 - axis_at))
    return level


def assign_block(rng, own, number, rows, count, top, limit, slope):
    sequence = jax.random.permutation(rng, count)
    packed, ordinary = portions_of(count, rows * top, limit, slope, True), portions_of(count, rows * top, limit, slope, False)
    places = jnp.arange(count)

    def named(sizes, rotation):
        used = int((sizes > 0).sum())
        fixed = max(1, used // 4)
        passed = fixed + (places - fixed + rotation * (used - fixed)) % max(1, count - fixed)
        return jnp.zeros((count,), jnp.int32).at[sequence[jnp.where(places < fixed, places, passed)]].set(jnp.asarray(sizes, jnp.int32))

    sizes = jnp.where(number % 4 == 0, named(packed, number // 4), named(ordinary, number - number // 4 - 1))
    mixed = jax.random.permutation(jax.random.fold_in(own, 3), count)
    giver, receiver = mixed[0:count // 2 * 2:2], mixed[1:count // 2 * 2:2]
    slack = jnp.minimum(sizes[giver] - 1, limit - sizes[receiver]) // 2
    slack = jnp.where((giver == sequence[0]) | (receiver == sequence[0]) | (sizes[receiver] == 0), 0, jnp.maximum(slack, 0))
    passed = jax.random.randint(jax.random.fold_in(own, 4), (count // 2,), 0, 1 << 20) % (slack + 1)
    sizes = sizes.at[giver].add(-passed).at[receiver].add(passed)
    members = jnp.searchsorted(jnp.cumsum(sizes), jnp.arange(rows * top), side="right").astype(jnp.int32)
    listing = members.reshape(top, rows).T
    listing = listing[jax.random.permutation(jax.random.fold_in(own, 1), rows)]
    rotation = jax.random.randint(jax.random.fold_in(own, 2), (rows, 1), 0, top)
    return jnp.take_along_axis(listing, (jnp.arange(top)[None, :] + rotation) % top, axis=1)


def portions_of(number_of, total, reach, slope, full):
    portions = [(1 << 20) // math.isqrt(rank ** slope) + 1 for rank in range(1, number_of + 1)]
    largest = reach if full else min(reach, max(-(-total // number_of), total * portions[0] // sum(portions)))
    least = 1 if total - largest >= number_of - 1 else 0
    holding, surplus = [largest] + [least] * (number_of - 1), total - largest - least * (number_of - 1)
    while surplus > 0:
        candidates = [i for i in range(1, number_of) if holding[i] < largest] or [i for i in range(1, number_of) if holding[i] < reach]
        whole, remaining = sum([portions[i] for i in candidates]), surplus
        for i in candidates:
            more = min(reach - holding[i], max(1, remaining * portions[i] // whole), surplus)
            holding[i] = holding[i] + more
            surplus = surplus - more
    return np.array(holding)


def noise(key, shape, scale, limit, pieces=(), held_as=jnp.bfloat16):
    array = scale * jax.random.normal(key, shape, jnp.float32)
    if pieces:
        array = array * steps_of(key, shape, pieces, -0.22, 0.18)
    return jnp.clip(array, -limit, limit).astype(held_as)


def setup_inputs(seed: int = 0) -> dict:
    streams_of = jax.random.split(jax.random.key(seed), 6)
    block_sums = noise(streams_of[0], (BLOCKS, BAND, COLS), 1.0, 6.0, ((0, 32),), jnp.float32)
    block_weights = jnp.clip(jnp.exp(math.log(2.0) - 2.9957323 * jax.random.uniform(streams_of[1], (BLOCKS, BAND, COLS), jnp.float32) ** steps_of(streams_of[1], (BLOCKS, BAND, COLS), ((0, 32),), -0.2, 0.2)), 0.1, 2.0)
    block_tile_keys = jax.random.split(jax.random.fold_in(streams_of[2], 1), BLOCKS // BLK_DEV)
    block_tile_turns = jax.random.permutation(jax.random.fold_in(streams_of[2], 3), BLOCKS // BLK_DEV)
    block_tile = jax.vmap(lambda own, number: assign_block(jax.random.fold_in(streams_of[2], 2), own, number, BLK_DEV, DEVICES, 1, CAP, 2))(block_tile_keys, block_tile_turns).reshape((BLOCKS, 1))
    block_row = set_ends(jax.random.randint(streams_of[3], (BLOCKS,), 0, BLK_DEV), jax.random.fold_in(streams_of[3], 1), 0, BLK_DEV - 1).astype(jnp.int32)
    prior_weight = jnp.clip(jnp.exp(math.log(1.0) - 2.3025851 * jax.random.uniform(streams_of[4], (NY, NX), jnp.float32) ** steps_of(streams_of[4], (NY, NX), ((0, 4), (1, 8)), -0.2, 0.2)), 0.1, 1.0)
    return dict(block_sums=block_sums, block_weights=block_weights, block_tile=block_tile, block_row=block_row, prior_weight=prior_weight)


def kernel_taps():
    dist = jnp.abs(jnp.arange(-HALF, HALF + 1).astype(jnp.float32))
    scaled = dist / (HALF + 1.0)
    taps = (1.0 - scaled) ** 4 * (1.0 + 4.0 * scaled)
    return taps / jnp.sum(taps)

def smooth(field, taps):
    image = field[None, None]
    image = lax.conv_general_dilated(image, taps[None, None, :, None], (1, 1), [(HALF, HALF), (0, 0)], precision=lax.Precision.HIGHEST)
    image = lax.conv_general_dilated(image, taps[None, None, None, :], (1, 1), [(0, 0), (HALF, HALF)], precision=lax.Precision.HIGHEST)
    return image[0, 0]

def reference(block_sums, block_weights, block_tile, block_row, prior_weight):
    total_blocks = block_sums.shape[0]
    zeros = jnp.zeros((NY, NX), jnp.float32)

    def place(index, carry):
        sums, weights = carry
        target = block_tile[index, 0].astype(jnp.int32)
        top = (target // N_TX * ROWS + block_row[index] * BAND).astype(jnp.int32)
        left = (target % N_TX * COLS).astype(jnp.int32)
        old_sums = lax.dynamic_slice(sums, (top, left), (BAND, COLS))
        old_weights = lax.dynamic_slice(weights, (top, left), (BAND, COLS))
        sums = lax.dynamic_update_slice(sums, old_sums + block_sums[index], (top, left))
        weights = lax.dynamic_update_slice(weights, old_weights + block_weights[index], (top, left))
        return (sums, weights)
    cell_sums, cell_weights = lax.fori_loop(0, total_blocks, place, (zeros, zeros))
    root = jnp.sqrt(prior_weight + cell_weights)
    right_side = cell_sums / root
    taps = kernel_taps()

    def operate(field):
        return 0.5 * field + root * smooth(root * field, taps)
    solution_field = jnp.zeros_like(right_side)
    residual, direction = (right_side, right_side)
    norm_now = jnp.sum(residual * residual)
    for step in range(ITERS):
        image = operate(direction)
        alpha = norm_now / jnp.sum(direction * image)
        solution_field = solution_field + alpha * direction
        residual = residual - alpha * image
        norm_next = jnp.sum(residual * residual)
        direction = residual + norm_next / norm_now * direction
        norm_now = norm_next
    return (solution_field, residual)
```

```python
import functools

import jax
import jax.numpy as jnp
import numpy as np
from jax import lax
from jax.experimental import pallas as pl
from jax.experimental.pallas import tpu as pltpu
from jax.sharding import PartitionSpec as P

HALF = 32
LANES = 128
PIECES = 5
LIMIT = 20 * 1024 * 1024
MESH = pl.DeviceIdType.MESH


def taps_matrix(offset):
    def weight(distance):
        scaled = np.abs(distance) / (HALF + 1.0)
        value = (1.0 - scaled) ** 4 * (1.0 + 4.0 * scaled)
        return np.where(np.abs(distance) <= HALF, value, 0.0)

    total = np.sum(weight(np.arange(-HALF, HALF + 1).astype(np.float64)))
    return (weight(offset.astype(np.float64)) / total).astype(np.float32)


def halves(values):
    high = values.astype(jnp.bfloat16)
    return high, (values - high.astype(jnp.float32)).astype(jnp.bfloat16)


def kernel_matrices(rows, width):
    row = np.arange(rows)[:, None] - (np.arange(rows + 2 * HALF)[None, :] - HALF)
    col = (np.arange(width + 2 * LANES)[:, None] - LANES) - np.arange(width)[None, :]
    row_high, row_low = halves(jnp.asarray(taps_matrix(row)))
    col_high, col_low = halves(jnp.asarray(taps_matrix(col)))
    return jnp.concatenate([row_high, row_low], axis=0), col_high, col_low


def directions():
    return [(dy, dx) for dy in (-1, 0, 1) for dx in (-1, 0, 1) if (dy, dx) != (0, 0)]


def span(step, size, margin, width, sending):
    if step == 0:
        return pl.ds(margin, size)
    if sending:
        return pl.ds(margin, width) if step < 0 else pl.ds(margin + size - width, width)
    return pl.ds(margin + size, width) if step < 0 else pl.ds(margin - width, width)


def dot(left, right):
    return jnp.dot(left, right, preferred_element_type=jnp.float32)


def cross(left, right):
    return lax.dot_general(
        left, right, (((0,), (0,)), ((), ())), preferred_element_type=jnp.float32
    )


def iota(shape, dim):
    return lax.broadcasted_iota(jnp.int32, shape, dim)


def ones(mask):
    return jnp.where(mask, 1.0, 0.0).astype(jnp.bfloat16)


def total(values):
    return jnp.sum(values, axis=(0, 1), keepdims=True)


def solve_kernel(
    ny,
    nx,
    slots,
    direct,
    room,
    tile_hbm,
    band_hbm,
    sums_hbm,
    weights_hbm,
    prior_hbm,
    row_hbm,
    col_high_hbm,
    col_low_hbm,
    r0_ref,
    u_ref,
    z_ref,
    scalars_ref,
    tile_ref,
    band_ref,
    sums_ref,
    weights_ref,
    prior_ref,
    row_ref,
    col_high_ref,
    col_low_ref,
    root_ref,
    load_sem,
    send_table,
    got_table,
    send_near,
    got_near,
    send_far,
    got_far,
    send_spill,
    got_spill,
    send_relay,
    got_relay,
    send_list,
    got_list,
    pad_a,
    pad_b,
    part,
    parts,
    table_sem,
    near_sem,
    far_sem,
    spill_sem,
    relay_sem,
    halo_send,
    halo_recv,
    part_sem,
):
    count = ny * nx
    side_x = nx // 2
    flat_x = side_x // 2
    peers = ny * side_x
    spill = slots - direct
    blocks, groups, _ = sums_ref.shape
    rows, cols = prior_ref.shape
    width = col_high_ref.shape[1]
    ty, tx = lax.axis_index("ty"), lax.axis_index("tx")
    me = ty * nx + tx
    side = tx // side_x
    inner_x = lax.rem(tx, side_x)
    here = ty * side_x + inner_x
    far_side = 1 - side

    def device(index):
        hop = index // ny
        sign = 1 - 2 * lax.rem(hop, 2)
        other_x = lax.rem(tx + nx // 2 + nx + sign * ((hop + 1) // 2), nx)
        return lax.rem(ty + ny // 2 + index, ny), other_x

    barrier = pltpu.get_barrier_semaphore()

    def greet(index, carry):
        other_y, other_x = device(index)

        @pl.when(other_y * nx + other_x != me)
        def _():
            pl.semaphore_signal(
                barrier, inc=1, device_id=(other_y, other_x), device_id_type=MESH
            )

        return carry

    loads = [
        pltpu.make_async_copy(source, target, load_sem.at[index])
        for index, (source, target) in enumerate(
            (
                (tile_hbm, tile_ref),
                (band_hbm, band_ref),
                (sums_hbm, sums_ref),
                (weights_hbm, weights_ref),
                (row_hbm, row_ref),
                (col_high_hbm, col_high_ref),
                (col_low_hbm, col_low_ref),
                (prior_hbm, prior_ref),
            )
        )
    ]
    for load in loads[:4]:
        load.start()
    for pad in (pad_a, pad_b):
        pad[0:HALF, :] = jnp.zeros((HALF, cols + 2 * LANES), jnp.float32)
        pad[HALF + rows :, :] = jnp.zeros((HALF, cols + 2 * LANES), jnp.float32)
        pad[HALF : HALF + rows, 0:LANES] = jnp.zeros((rows, LANES), jnp.float32)
        pad[HALF : HALF + rows, LANES + cols :] = jnp.zeros((rows, LANES), jnp.float32)
    lax.fori_loop(0, count, greet, 0)
    for load in loads[4:]:
        load.start()

    loads[0].wait()
    loads[1].wait()
    tile = tile_ref[...]
    square = (blocks, blocks)
    down, across = iota(square, 0), iota(square, 1)

    def as_column(row):
        spread = jnp.broadcast_to(row, square)
        return jnp.sum(jnp.where(down == across, spread, 0), axis=1, keepdims=True)

    def before(column):
        return jnp.sum(jnp.where(down < across, column, 0), axis=0, keepdims=True)

    def before_column(row):
        return jnp.sum(jnp.where(across < down, row, 0), axis=1, keepdims=True)

    def seat(tiles):
        return tiles // nx * side_x + lax.rem(tiles, side_x)

    def crosses(tiles):
        return lax.rem(tiles, nx) // side_x != side

    tile_column = as_column(tile)
    same = jnp.where(tile_column == tile, 1, 0)
    rank, rank_column = before(same), before_column(same)
    near_rows, far_rows = peers * slots, peers * direct
    index = jnp.where(
        crosses(tile),
        near_rows + seat(tile) * direct + rank,
        seat(tile) * slots + rank,
    )
    if spill:
        over = jnp.where(crosses(tile) & (rank >= direct), 1, 0)
        over_column = jnp.where(crosses(tile_column) & (rank_column >= direct), 1, 0)
        turn = before(over_column)
        index = jnp.where(over > 0, jnp.where(turn < room, near_rows + far_rows + turn, -1), index)
        turn_column = before_column(over)
        listing = jnp.where(
            (turn_column == iota((blocks, LANES), 1)) & (over_column > 0),
            seat(tile_column) * spill + rank_column - direct + 1,
            0,
        )
        send_list[...] = jnp.sum(listing, axis=0, keepdims=True).astype(jnp.float32)
        excess = jnp.sum(over, axis=1, keepdims=True).astype(jnp.float32)
    place = ones(iota((near_rows + far_rows + room, blocks), 0) == index)
    place = jnp.concatenate([place, place], axis=1)
    owner = ones(iota((count, blocks), 0) == tile)
    numbers = jnp.where(
        rank_column == iota((blocks, LANES), 1), as_column(band_ref[...]) + 1, 0
    ).astype(jnp.float32)
    table = dot(owner, numbers.astype(jnp.bfloat16))
    if spill:
        table = jnp.where(iota((count, LANES), 1) == LANES - 1, excess, table)
    send_table[...] = table.reshape(count, 1, LANES)

    def pack(source, array):
        for group in range(0, groups, 2):
            window = slice(group * LANES, (group + 2) * LANES)
            values = jnp.concatenate([source[:, group, :], source[:, group + 1, :]], axis=1)
            moved = dot(place, jnp.concatenate(halves(values), axis=0))
            send_near[array, :, :, window] = moved[:near_rows].reshape(peers, slots, 2 * LANES)
            moved = moved[near_rows:]
            send_far[array, :, :, window] = moved[:far_rows].reshape(peers, direct, 2 * LANES)
            if spill:
                send_spill[array, :, window] = moved[far_rows:]

    def push(source, target, semaphores, which, other_y, other_x):
        pltpu.make_async_remote_copy(
            src_ref=source,
            dst_ref=target,
            send_sem=semaphores.at[0, which],
            recv_sem=semaphores.at[1, which],
            device_id=(other_y, other_x),
            device_id_type=MESH,
        ).start()

    def cut(ref, place, window):
        return ref.at[place] if window is None else ref.at[place, :, window]

    def route(source, target, semaphores, which, reach, window=None):
        def send(index, carry):
            other_y = lax.rem(ty + ny // 2 + index, ny)
            hop = index // ny
            if reach == "far":
                inner = lax.rem(inner_x + side_x // 2 + hop, side_x)
                other_x = inner + side_x * far_side
            else:
                layer = inner_x // flat_x
                layer = layer if reach == "flat" else 1 - layer
                inner = layer * flat_x + lax.rem(inner_x + flat_x // 2 + hop, flat_x)
                other_x = inner + side_x * side
            there = other_y * side_x + inner

            def go():
                push(
                    cut(source, there, window),
                    cut(target, here, window),
                    semaphores,
                    which,
                    other_y,
                    other_x,
                )

            if reach == "flat":
                pl.when(there != here)(go)
            else:
                go()
            return carry

        lax.fori_loop(0, peers if reach == "far" else ny * flat_x, send, 0)

    def share(source_of, target, semaphores):
        def send(index, carry):
            other_y, other_x = device(index)
            other = other_y * nx + other_x

            @pl.when(other != me)
            def _():
                push(source_of(other), target.at[me], semaphores, 0, other_y, other_x)

            return carry

        lax.fori_loop(0, count, send, 0)

    def mirror(source, target, semaphores, which):
        push(source, target, semaphores, which, ty, inner_x + side_x * far_side)

    def drain(ref, semaphores, way, which):
        pltpu.make_async_copy(ref, ref, semaphores.at[way, which]).wait()

    def arrived(target, semaphores, which, number, window=None, way=1):
        drain(cut(target, pl.ds(0, number), window), semaphores, way, which)

    def exchange(pad, phase, start, size):
        copies = []
        for index, (dy, dx) in enumerate(directions()):
            if (dx < 0 and start > 0) or (dx > 0 and start + size < cols):
                continue
            middle = pl.ds(LANES + start, size)
            copy = pltpu.make_async_remote_copy(
                src_ref=pad.at[
                    span(dy, rows, HALF, HALF, True),
                    span(dx, cols, LANES, LANES, True) if dx else middle,
                ],
                dst_ref=pad.at[
                    span(dy, rows, HALF, HALF, False),
                    span(dx, cols, LANES, LANES, False) if dx else middle,
                ],
                send_sem=halo_send.at[phase, index],
                recv_sem=halo_recv.at[phase, index],
                device_id=(
                    lax.rem(ty + dy + ny, ny),
                    lax.rem(tx + dx + nx, nx),
                ),
                device_id_type=MESH,
            )
            goes = (ty + dy >= 0) & (ty + dy < ny) & (tx + dx >= 0) & (tx + dx < nx)
            comes = (ty - dy >= 0) & (ty - dy < ny) & (tx - dx >= 0) & (tx - dx < nx)
            copies.append((copy, goes, comes))
            pl.when(goes)(copy.start)
        return copies

    def receive(copies):
        for copy, goes, comes in copies:
            pl.when(comes)(copy.wait_recv)

    def finish(copies):
        for copy, goes, comes in copies:
            pl.when(goes)(copy.wait_send)

    def smooth(pad):
        high, low = halves(pad[...])
        both = dot(row_ref[...], high)
        down = both[:rows] + both[rows:] + dot(row_ref[0:rows, :], low)
        high, low = halves(down)
        stacked = jnp.concatenate([high, low], axis=0)
        pieces = []
        for left in range(0, cols, width):
            window = slice(left, left + width + 2 * LANES)
            both = dot(stacked[:, window], col_high_ref[...])
            pieces.append(both[:rows] + both[rows:] + dot(high[:, window], col_low_ref[...]))
        return jnp.concatenate(pieces, axis=1)

    quarter, eighth = cols // 4, cols // 8
    cuts = [(0, quarter), (3 * quarter, quarter), (quarter, quarter)]
    cuts += [(2 * quarter, eighth), (2 * quarter + eighth, eighth)]
    windows = [pl.ds(start, size) for start, size in cuts]

    def supply(piece):
        route(send_far.at[1], got_far.at[1], far_sem, 1 + piece, "far", windows[piece])

    def supply_near(array, reach, which, window=None):
        route(send_near.at[array], got_near.at[array], near_sem, which, reach, window)

    def settle_flat(ref, array, semaphores, which, way=1):
        arrived(ref.at[array], semaphores, which, ny * flat_x - 1, way=way)

    def settle_rise(ref, array, semaphores, which, window=None, way=1):
        arrived(ref.at[array], semaphores, which, ny * flat_x, window, way=way)

    loads[2].wait()
    pack(sums_ref, 0)
    loads[3].wait()
    pack(weights_ref, 1)
    pl.semaphore_wait(barrier, count - 1)
    if spill:
        mirror(send_list, got_list, spill_sem, 2)
        mirror(send_spill.at[0], got_spill.at[0], spill_sem, 0)
    share(lambda other: send_table.at[other], got_table, table_sem)
    supply_near(0, "rise", 1)
    route(send_far.at[0], got_far.at[0], far_sem, 0, "far")
    supply_near(0, "flat", 0)
    supply_near(1, "flat", 2)
    got_table[pl.ds(me, 1)] = send_table[pl.ds(me, 1)]
    for array in range(2):
        got_near[array, pl.ds(here, 1)] = send_near[array, pl.ds(here, 1)]

    def supply_relay(array, reach, which, window=None):
        route(send_relay.at[array], got_relay.at[array], relay_sem, which, reach, window)

    def relay(array):
        drain(got_spill.at[array], spill_sem, 1, array)
        moved = dot(hand, jnp.concatenate(halves(got_spill[array]), axis=0))
        send_relay[array] = moved.reshape(peers, spill, cols)
        got_relay[array, pl.ds(here, 1)] = send_relay[array, pl.ds(here, 1)]

    if spill:
        drain(got_list, spill_sem, 1, 2)
        named = got_list[...][:, :room]
        hand = ones(iota((peers * spill, room), 0).astype(jnp.float32) + 1.0 == named)
        hand = jnp.concatenate([hand, hand], axis=1)
        relay(0)
        supply_relay(0, "rise", 1)
        supply_relay(0, "flat", 0)
        mirror(send_spill.at[1], got_spill.at[1], spill_sem, 1)

    arrived(got_table, table_sem, 0, count - 1)
    slot = iota((1, count * slots), 1)
    past = slot - near_rows
    line = jnp.where(past < 0, slot // slots, past // direct)
    rank = jnp.where(past < 0, lax.rem(slot, slots), lax.rem(past, direct))
    if spill:
        later = past - far_rows
        line = jnp.where(later < 0, line, later // spill)
        rank = jnp.where(later < 0, rank, direct + lax.rem(later, spill))
    origin = line // side_x * nx + lax.rem(line, side_x)
    origin = origin + side_x * jnp.where(past < 0, side, far_side)
    table = got_table[...].reshape(count, LANES)
    listed = cross(table.astype(jnp.bfloat16), ones(iota((count, count * slots), 0) == origin))
    listed = jnp.where(iota(listed.shape, 0) == rank, listed, 0.0)
    listed = jnp.sum(listed, axis=0, keepdims=True)
    select = ones(iota((rows, count * slots), 0).astype(jnp.float32) + 1.0 == listed)

    def gather(array, window):
        def lines(ref, number):
            values = ref[array, :, :, window]
            return values.reshape(peers * number, values.shape[-1])

        values = [lines(got_near, slots), lines(got_far, direct)]
        if spill:
            values.append(lines(got_relay, spill))
        high, low = halves(jnp.concatenate(values, axis=0))
        return dot(select, high) + dot(select, low)

    settle_flat(got_near, 0, near_sem, 0)
    settle_rise(got_near, 0, near_sem, 1)
    arrived(got_far.at[0], far_sem, 0, peers)
    if spill:
        settle_flat(got_relay, 0, relay_sem, 0)
        settle_rise(got_relay, 0, relay_sem, 1)
    pad_a[HALF : HALF + rows, LANES : LANES + cols] = gather(0, slice(None))
    first = exchange(pad_a, 0, 0, cols)
    supply(0)
    supply_near(1, "rise", 3, windows[0])
    if spill:
        relay(1)
        supply_relay(1, "flat", 2)
    for piece, window in enumerate(windows):
        if piece > 0:
            supply_near(1, "rise", 3 + piece, window)
        if spill:
            supply_relay(1, "rise", 3 + piece, window)
        if piece > 0:
            supply(piece)
    for load in loads[4:]:
        load.wait()
    receive(first)
    u_ref[...] = smooth(pad_a)

    second = []
    settle_flat(got_near, 1, near_sem, 2)
    if spill:
        settle_flat(got_relay, 1, relay_sem, 2)
    for piece, window in enumerate(windows):
        left, size = cuts[piece]
        inner = slice(LANES + left, LANES + left + size)
        settle_rise(got_near, 1, near_sem, 3 + piece, window)
        if spill:
            settle_rise(got_relay, 1, relay_sem, 3 + piece, window)
        arrived(got_far.at[1], far_sem, 1 + piece, peers, window)
        root = jnp.sqrt(prior_ref[:, window] + gather(1, window))
        root_ref[:, window] = root
        r0_ref[:, window] = pad_a[HALF : HALF + rows, inner] / root
        u = root * u_ref[:, window]
        u_ref[:, window] = u
        pad_b[HALF : HALF + rows, inner] = root * u
        second += exchange(pad_b, 1 + piece, left, size)
    r0, u = r0_ref[...], u_ref[...]
    rr, ru = total(r0 * r0), total(r0 * u)
    own = jnp.where(rr > 0.0, ru / rr, 0.0)
    receive(second)
    z = root_ref[...] * smooth(pad_b)
    z_ref[...] = z
    q = own * r0 - u
    g = own * u - z
    lane = iota((1, LANES), 1)
    packed = jnp.zeros((1, LANES), jnp.float32)
    for index, value in enumerate((rr, ru, total(q * q), total(q * g), total(r0 * g))):
        packed = jnp.where(lane == index, value, packed)
    part[...] = packed
    parts[pl.ds(me, 1), 0, :] = packed
    share(lambda other: part, parts, part_sem)
    arrived(parts, part_sem, 0, count - 1)

    table = parts[...].reshape(count, LANES)
    rr_d, ru_d, qq_d, qg_d, rg_d = [table[:, i : i + 1] for i in range(5)]
    rr, ru = total(rr_d), total(ru_d)
    mu = ru / rr
    shift = mu - jnp.where(rr_d > 0.0, ru_d / rr_d, 0.0)
    qq = total(qq_d + shift * shift * rr_d)
    qg = total(qg_d + shift * (rg_d - qq_d) + shift * shift * ru_d)
    alpha0 = rr / (0.5 * rr + ru)
    norm = alpha0 * alpha0 * qq
    beta = norm / rr
    alpha1 = norm / (alpha0 * alpha0 * (0.5 * qq + qg) - beta * norm / alpha0)
    most = jnp.zeros((1, 1), jnp.float32)
    if spill:
        most = jnp.max(got_table[...].reshape(count, LANES), axis=0, keepdims=True)[:, LANES - 1 :]
    flag = jnp.where(most > room, 1.0, 0.0)
    packed = jnp.zeros((1, LANES), jnp.float32)
    for index, value in enumerate((alpha0, alpha1, beta, mu, flag)):
        packed = jnp.where(lane == index, value, packed)
    scalars_ref[...] = packed

    finish(first)
    finish(second)
    arrived(send_table, table_sem, 0, count - 1, way=0)
    for array in range(2):
        settle_flat(send_near, array, near_sem, 2 * array, way=0)
    settle_rise(send_near, 0, near_sem, 1, way=0)
    arrived(send_far.at[0], far_sem, 0, peers, way=0)
    for piece, window in enumerate(windows):
        arrived(send_far.at[1], far_sem, 1 + piece, peers, window, way=0)
        settle_rise(send_near, 1, near_sem, 3 + piece, window, way=0)
        if spill:
            settle_rise(send_relay, 1, relay_sem, 3 + piece, window, way=0)
    if spill:
        drain(send_list, spill_sem, 0, 2)
        for array in range(2):
            drain(send_spill.at[array], spill_sem, 0, array)
            settle_flat(send_relay, array, relay_sem, 2 * array, way=0)
        settle_rise(send_relay, 0, relay_sem, 1, way=0)
    arrived(parts, part_sem, 0, count - 1, way=0)


def close_kernel(r0_ref, u_ref, z_ref, scalars_ref, field_ref, residual_ref):
    alpha0, alpha1, beta, mu = [scalars_ref[0:1, i : i + 1] for i in range(4)]
    r0, u = r0_ref[...], u_ref[...]
    q = mu * r0 - u
    r1 = alpha0 * q
    field_ref[...] = alpha0 * r0 + alpha1 * (r1 + beta * r0)
    along = alpha0 * (0.5 * q + mu * u - z_ref[...]) + beta * (0.5 * r0 + u)
    residual_ref[...] = r1 - alpha1 * along


def solve(slots, direct, room, identity, arrays):
    ny, nx = lax.axis_size("ty"), lax.axis_size("tx")
    block_tile, block_row, block_sums, block_weights, prior_weight, *matrices = arrays
    count = ny * nx
    blocks, groups, _ = block_sums.shape
    rows, cols = prior_weight.shape
    peers = count // 2
    spill = max(slots - direct, 1)
    vmem = pl.BlockSpec(memory_space=pltpu.VMEM)
    hbm = pl.BlockSpec(memory_space=pltpu.HBM)
    shape = jax.ShapeDtypeStruct((rows, cols), jnp.float32)

    def scratch(*shape):
        return pltpu.VMEM(shape, jnp.float32)

    def semaphores(*shape):
        return pltpu.SemaphoreType.DMA(shape)

    def twice(*shape):
        return [scratch(*shape), scratch(*shape)]

    return pl.pallas_call(
        functools.partial(solve_kernel, ny, nx, slots, direct, room),
        out_shape=(shape, shape, shape, jax.ShapeDtypeStruct((1, LANES), jnp.float32)),
        in_specs=[hbm] * 8,
        out_specs=(vmem,) * 4,
        scratch_shapes=[
            pltpu.VMEM((1, blocks), jnp.int32),
            pltpu.VMEM((1, blocks), jnp.int32),
            *twice(blocks, groups, LANES),
            scratch(rows, cols),
            *[pltpu.VMEM(matrix.shape, matrix.dtype) for matrix in matrices],
            scratch(rows, cols),
            semaphores(8),
            *twice(count, 1, LANES),
            *twice(2, peers, slots, cols),
            *twice(2, peers, direct, cols),
            *twice(2, max(room, 8), cols),
            *twice(2, peers, spill, cols),
            *twice(1, LANES),
            *twice(rows + 2 * HALF, cols + 2 * LANES),
            scratch(1, LANES),
            scratch(count, 1, LANES),
            semaphores(2, 1),
            semaphores(2, 3 + PIECES),
            semaphores(2, 1 + PIECES),
            semaphores(2, 3),
            semaphores(2, 3 + PIECES),
            semaphores(1 + PIECES, 8),
            semaphores(1 + PIECES, 8),
            semaphores(2, 1),
        ],
        compiler_params=pltpu.CompilerParams(
            collective_id=identity, has_side_effects=True, vmem_limit_bytes=LIMIT
        ),
    )(*[pltpu.with_memory_space_constraint(array, pltpu.HBM) for array in arrays])


def close(r0, u, z, scalars):
    vmem = pl.BlockSpec(memory_space=pltpu.VMEM)
    shape = jax.ShapeDtypeStruct(r0.shape, jnp.float32)
    return pl.pallas_call(
        close_kernel, out_shape=(shape, shape), in_specs=[vmem] * 4, out_specs=(vmem, vmem),
        compiler_params=pltpu.CompilerParams(vmem_limit_bytes=LIMIT),
    )(r0, u, z, scalars)


def shards(block_sums, block_weights, block_tile, block_row, prior_weight):
    count = lax.axis_size("ty") * lax.axis_size("tx")
    blocks, band, cols = block_sums.shape
    slots = 2 * blocks // count
    arrays = (
        block_tile.reshape(1, blocks),
        block_row.reshape(1, blocks),
        block_sums.reshape(blocks * band, cols // LANES, LANES),
        block_weights.reshape(blocks * band, cols // LANES, LANES),
        prior_weight,
        *kernel_matrices(prior_weight.shape[0], 2 * LANES),
    )
    fields = solve(slots, slots // 2, blocks // 4, 0, arrays)
    return lax.cond(
        fields[3][0, 4] > 0.5,
        lambda fields: close(*solve(slots, slots, 0, 1, arrays)),
        lambda fields: close(*fields),
        fields,
    )


def solution(mesh):
    in_specs = (
        P(("ty", "tx"), None, None),
        P(("ty", "tx"), None, None),
        P(("ty", "tx"), None),
        P(("ty", "tx")),
        P("ty", "tx"),
    )
    out_specs = (P("ty", "tx"), P("ty", "tx"))
    return jax.shard_map(shards, mesh=mesh, in_specs=in_specs, out_specs=out_specs, check_vma=False)
```

```python
import functools

import jax
import jax.numpy as jnp
import numpy as np
from jax import lax
from jax.experimental import pallas as pl
from jax.experimental.pallas import tpu as pltpu
from jax.sharding import PartitionSpec as P

HALF = 32
LANES = 128
PIECES = 4
EARLY = 2
AHEAD = 1
LIMIT = 20 * 1024 * 1024
MESH = pl.DeviceIdType.MESH


def taps_matrix(offset):
    def weight(distance):
        scaled = np.abs(distance) / (HALF + 1.0)
        value = (1.0 - scaled) ** 4 * (1.0 + 4.0 * scaled)
        return np.where(np.abs(distance) <= HALF, value, 0.0)

    total = np.sum(weight(np.arange(-HALF, HALF + 1).astype(np.float64)))
    return (weight(offset.astype(np.float64)) / total).astype(np.float32)


def halves(values):
    high = values.astype(jnp.bfloat16)
    return high, (values - high.astype(jnp.float32)).astype(jnp.bfloat16)


def kernel_matrices(rows, width):
    row = np.arange(rows)[:, None] - (np.arange(rows + 2 * HALF)[None, :] - HALF)
    col = (np.arange(width + 2 * LANES)[:, None] - LANES) - np.arange(width)[None, :]
    row_high, row_low = halves(jnp.asarray(taps_matrix(row)))
    col_high, col_low = halves(jnp.asarray(taps_matrix(col)))
    return jnp.concatenate([row_high, row_low], axis=0), col_high, col_low


def directions():
    return [(dy, dx) for dy in (-1, 0, 1) for dx in (-1, 0, 1) if (dy, dx) != (0, 0)]


def span(step, size, margin, width, sending):
    if step == 0:
        return pl.ds(margin, size)
    if sending:
        return pl.ds(margin, width) if step < 0 else pl.ds(margin + size - width, width)
    return pl.ds(margin + size, width) if step < 0 else pl.ds(margin - width, width)


def dot(left, right):
    return jnp.dot(left, right, preferred_element_type=jnp.float32)


def cross(left, right):
    return lax.dot_general(
        left, right, (((0,), (0,)), ((), ())), preferred_element_type=jnp.float32
    )


def iota(shape, dim):
    return lax.broadcasted_iota(jnp.int32, shape, dim)


def ones(mask):
    return jnp.where(mask, 1.0, 0.0).astype(jnp.bfloat16)


def total(values):
    return jnp.sum(values, axis=(0, 1), keepdims=True)


def solve_kernel(
    ny,
    nx,
    slots,
    direct,
    room,
    tile_hbm,
    band_hbm,
    sums_hbm,
    weights_hbm,
    prior_hbm,
    row_hbm,
    col_high_hbm,
    col_low_hbm,
    r0_ref,
    u_ref,
    z_ref,
    scalars_ref,
    tile_ref,
    band_ref,
    sums_ref,
    weights_ref,
    prior_ref,
    row_ref,
    col_high_ref,
    col_low_ref,
    root_ref,
    load_sem,
    send_table,
    got_table,
    send_near,
    got_near,
    send_far,
    got_far,
    send_spill,
    got_spill,
    send_relay,
    got_relay,
    send_list,
    got_list,
    pad_a,
    pad_b,
    part,
    parts,
    table_sem,
    near_sem,
    far_sem,
    spill_sem,
    relay_sem,
    halo_send,
    halo_recv,
    part_sem,
):
    count = ny * nx
    side_x = nx // 2
    flat_x = side_x // 2
    peers = ny * side_x
    spill = slots - direct
    blocks, groups, _ = sums_ref.shape
    rows, cols = prior_ref.shape
    width = col_high_ref.shape[1]
    ty, tx = lax.axis_index("ty"), lax.axis_index("tx")
    me = ty * nx + tx
    side = tx // side_x
    inner_x = lax.rem(tx, side_x)
    here = ty * side_x + inner_x
    far_side = 1 - side

    def device(index):
        hop = index // ny
        sign = 1 - 2 * lax.rem(hop, 2)
        other_x = lax.rem(tx + nx // 2 + nx + sign * ((hop + 1) // 2), nx)
        return lax.rem(ty + ny // 2 + index, ny), other_x

    barrier = pltpu.get_barrier_semaphore()

    def greet(index, carry):
        other_y, other_x = device(index)

        @pl.when(other_y * nx + other_x != me)
        def _():
            pl.semaphore_signal(
                barrier, inc=1, device_id=(other_y, other_x), device_id_type=MESH
            )

        return carry

    loads = [
        pltpu.make_async_copy(source, target, load_sem.at[index])
        for index, (source, target) in enumerate(
            (
                (tile_hbm, tile_ref),
                (band_hbm, band_ref),
                (sums_hbm, sums_ref),
                (weights_hbm, weights_ref),
                (row_hbm, row_ref),
                (col_high_hbm, col_high_ref),
                (col_low_hbm, col_low_ref),
                (prior_hbm, prior_ref),
            )
        )
    ]
    lax.fori_loop(0, count, greet, 0, unroll=True)
    for load in loads[:4]:
        load.start()
    for pad in (pad_a, pad_b):
        pad[0:HALF, :] = jnp.zeros((HALF, cols + 2 * LANES), jnp.float32)
        pad[HALF + rows :, :] = jnp.zeros((HALF, cols + 2 * LANES), jnp.float32)
        pad[HALF : HALF + rows, 0:LANES] = jnp.zeros((rows, LANES), jnp.float32)
        pad[HALF : HALF + rows, LANES + cols :] = jnp.zeros((rows, LANES), jnp.float32)
    for load in loads[4:]:
        load.start()

    loads[0].wait()
    loads[1].wait()
    tile = tile_ref[...]
    square = (blocks, blocks)
    down, across = iota(square, 0), iota(square, 1)

    def as_column(row):
        spread = jnp.broadcast_to(row, square)
        return jnp.sum(jnp.where(down == across, spread, 0), axis=1, keepdims=True)

    def before(column):
        return jnp.sum(jnp.where(down < across, column, 0), axis=0, keepdims=True)

    def before_column(row):
        return jnp.sum(jnp.where(across < down, row, 0), axis=1, keepdims=True)

    def seat(tiles):
        return tiles // nx * side_x + lax.rem(tiles, side_x)

    def crosses(tiles):
        return lax.rem(tiles, nx) // side_x != side

    tile_column = as_column(tile)
    same = jnp.where(tile_column == tile, 1, 0)
    rank, rank_column = before(same), before_column(same)
    near_rows, far_rows = peers * slots, peers * direct
    index = jnp.where(
        crosses(tile),
        near_rows + seat(tile) * direct + rank,
        seat(tile) * slots + rank,
    )
    if spill:
        over = jnp.where(crosses(tile) & (rank >= direct), 1, 0)
        over_column = jnp.where(crosses(tile_column) & (rank_column >= direct), 1, 0)
        turn = before(over_column)
        index = jnp.where(over > 0, jnp.where(turn < room, near_rows + far_rows + turn, -1), index)
        turn_column = before_column(over)
        listing = jnp.where(
            (turn_column == iota((blocks, LANES), 1)) & (over_column > 0),
            seat(tile_column) * spill + rank_column - direct + 1,
            0,
        )
        send_list[...] = jnp.sum(listing, axis=0, keepdims=True).astype(jnp.float32)
        excess = jnp.sum(over, axis=1, keepdims=True).astype(jnp.float32)
    place = ones(iota((near_rows + far_rows + room, blocks), 0) == index)
    place = jnp.concatenate([place, place], axis=1)
    owner = ones(iota((count, blocks), 0) == tile)
    numbers = jnp.where(
        rank_column == iota((blocks, LANES), 1), as_column(band_ref[...]) + 1, 0
    ).astype(jnp.float32)
    table = dot(owner, numbers.astype(jnp.bfloat16))
    if spill:
        table = jnp.where(iota((count, LANES), 1) == LANES - 1, excess, table)
    send_table[...] = table.reshape(count, 1, LANES)

    def pack(source, array):
        for group in range(0, groups, 2):
            window = slice(group * LANES, (group + 2) * LANES)
            values = jnp.concatenate([source[:, group, :], source[:, group + 1, :]], axis=1)
            moved = dot(place, jnp.concatenate(halves(values), axis=0))
            send_near[array, :, :, window] = moved[:near_rows].reshape(peers, slots, 2 * LANES)
            moved = moved[near_rows:]
            send_far[array, :, :, window] = moved[:far_rows].reshape(peers, direct, 2 * LANES)
            if spill:
                send_spill[array, :, window] = moved[far_rows:]

    def push(source, target, semaphores, which, other_y, other_x):
        pltpu.make_async_remote_copy(
            src_ref=source,
            dst_ref=target,
            send_sem=semaphores.at[0, which],
            recv_sem=semaphores.at[1, which],
            device_id=(other_y, other_x),
            device_id_type=MESH,
        ).start()

    def cut(ref, place, window):
        return ref.at[place] if window is None else ref.at[place, :, window]

    def route(source, target, semaphores, which, reach, window=None):
        def send(index, carry):
            other_y = lax.rem(ty + ny // 2 + index, ny)
            hop = index // ny
            if reach == "far":
                inner = lax.rem(inner_x + side_x // 2 + hop, side_x)
                other_x = inner + side_x * far_side
            else:
                layer = inner_x // flat_x
                layer = layer if reach == "flat" else 1 - layer
                inner = layer * flat_x + lax.rem(inner_x + flat_x // 2 + hop, flat_x)
                other_x = inner + side_x * side
            there = other_y * side_x + inner

            def go():
                push(
                    cut(source, there, window),
                    cut(target, here, window),
                    semaphores,
                    which,
                    other_y,
                    other_x,
                )

            if reach == "flat":
                pl.when(there != here)(go)
            else:
                go()
            return carry

        lax.fori_loop(0, peers if reach == "far" else ny * flat_x, send, 0, unroll=True)

    def share(source_of, target, semaphores):
        def send(index, carry):
            other_y, other_x = device(index)
            other = other_y * nx + other_x

            @pl.when(other != me)
            def _():
                push(source_of(other), target.at[me], semaphores, 0, other_y, other_x)

            return carry

        lax.fori_loop(0, count, send, 0, unroll=True)

    def mirror(source, target, semaphores, which):
        push(source, target, semaphores, which, ty, inner_x + side_x * far_side)

    def drain(ref, semaphores, way, which):
        pltpu.make_async_copy(ref, ref, semaphores.at[way, which]).wait()

    def arrived(target, semaphores, which, number, window=None, way=1):
        drain(cut(target, pl.ds(0, number), window), semaphores, way, which)

    def exchange(pad, phase, start, size):
        copies = []
        for index, (dy, dx) in enumerate(directions()):
            if (dx < 0 and start > 0) or (dx > 0 and start + size < cols):
                continue
            middle = pl.ds(LANES + start, size)
            copy = pltpu.make_async_remote_copy(
                src_ref=pad.at[
                    span(dy, rows, HALF, HALF, True),
                    span(dx, cols, LANES, LANES, True) if dx else middle,
                ],
                dst_ref=pad.at[
                    span(dy, rows, HALF, HALF, False),
                    span(dx, cols, LANES, LANES, False) if dx else middle,
                ],
                send_sem=halo_send.at[phase, index],
                recv_sem=halo_recv.at[phase, index],
                device_id=(
                    lax.rem(ty + dy + ny, ny),
                    lax.rem(tx + dx + nx, nx),
                ),
                device_id_type=MESH,
            )
            goes = (ty + dy >= 0) & (ty + dy < ny) & (tx + dx >= 0) & (tx + dx < nx)
            comes = (ty - dy >= 0) & (ty - dy < ny) & (tx - dx >= 0) & (tx - dx < nx)
            copies.append((copy, goes, comes))
            pl.when(goes)(copy.start)
        return copies

    def receive(copies):
        for copy, goes, comes in copies:
            pl.when(comes)(copy.wait_recv)

    def finish(copies):
        for copy, goes, comes in copies:
            pl.when(goes)(copy.wait_send)

    def smooth(pad):
        high, low = halves(pad[...])
        both = dot(row_ref[...], high)
        down = both[:rows] + both[rows:] + dot(row_ref[0:rows, :], low)
        high, low = halves(down)
        stacked = jnp.concatenate([high, low], axis=0)
        pieces = []
        for left in range(0, cols, width):
            window = slice(left, left + width + 2 * LANES)
            both = dot(stacked[:, window], col_high_ref[...])
            pieces.append(both[:rows] + both[rows:] + dot(high[:, window], col_low_ref[...]))
        return jnp.concatenate(pieces, axis=1)

    quarter, eighth = cols // 4, cols // 8
    cuts = [(0, quarter), (3 * quarter, quarter), (quarter, quarter), (2 * quarter, quarter)]
    windows = [pl.ds(start, size) for start, size in cuts]

    def supply_far(array, piece):
        which = array * PIECES + piece
        route(send_far.at[array], got_far.at[array], far_sem, which, "far", windows[piece])

    def supply_flat(source, target, semaphores, array):
        route(source.at[array], target.at[array], semaphores, array, "flat")

    def supply_rise(source, target, semaphores, array, piece):
        which = 2 + array * PIECES + piece
        route(source.at[array], target.at[array], semaphores, which, "rise", windows[piece])

    def settle_flat(ref, semaphores, array, way=1):
        arrived(ref.at[array], semaphores, array, ny * flat_x - 1, way=way)

    def settle_rise(ref, semaphores, array, piece, way=1):
        which = 2 + array * PIECES + piece
        arrived(ref.at[array], semaphores, which, ny * flat_x, windows[piece], way=way)

    def settle_far(ref, array, piece, way=1):
        arrived(ref.at[array], far_sem, array * PIECES + piece, peers, windows[piece], way=way)

    def settle_piece(array, piece):
        settle_rise(got_near, near_sem, array, piece)
        if spill:
            settle_rise(got_relay, relay_sem, array, piece)
        settle_far(got_far, array, piece)

    loads[2].wait()
    pack(sums_ref, 0)
    loads[3].wait()
    pack(weights_ref, 1)
    pl.semaphore_wait(barrier, count - 1)
    if spill:
        mirror(send_list, got_list, spill_sem, 2)
        mirror(send_spill.at[0], got_spill.at[0], spill_sem, 0)
    share(lambda other: send_table.at[other], got_table, table_sem)
    for piece in range(EARLY):
        supply_rise(send_near, got_near, near_sem, 0, piece)
        supply_far(0, piece)
    for array in range(2):
        supply_flat(send_near, got_near, near_sem, array)
    got_table[pl.ds(me, 1)] = send_table[pl.ds(me, 1)]
    for array in range(2):
        got_near[array, pl.ds(here, 1)] = send_near[array, pl.ds(here, 1)]

    def relay(array):
        drain(got_spill.at[array], spill_sem, 1, array)
        moved = dot(hand, jnp.concatenate(halves(got_spill[array]), axis=0))
        send_relay[array] = moved.reshape(peers, spill, cols)
        got_relay[array, pl.ds(here, 1)] = send_relay[array, pl.ds(here, 1)]

    if spill:
        drain(got_list, spill_sem, 1, 2)
        named = got_list[...][:, :room]
        hand = ones(iota((peers * spill, room), 0).astype(jnp.float32) + 1.0 == named)
        hand = jnp.concatenate([hand, hand], axis=1)
        relay(0)
        for piece in range(EARLY):
            supply_rise(send_relay, got_relay, relay_sem, 0, piece)
    for piece in range(EARLY, PIECES):
        supply_rise(send_near, got_near, near_sem, 0, piece)
        if spill:
            supply_rise(send_relay, got_relay, relay_sem, 0, piece)
        supply_far(0, piece)
    if spill:
        supply_flat(send_relay, got_relay, relay_sem, 0)
        mirror(send_spill.at[1], got_spill.at[1], spill_sem, 1)

    arrived(got_table, table_sem, 0, count - 1)
    slot = iota((1, count * slots), 1)
    past = slot - near_rows
    line = jnp.where(past < 0, slot // slots, past // direct)
    rank = jnp.where(past < 0, lax.rem(slot, slots), lax.rem(past, direct))
    if spill:
        later = past - far_rows
        line = jnp.where(later < 0, line, later // spill)
        rank = jnp.where(later < 0, rank, direct + lax.rem(later, spill))
    origin = line // side_x * nx + lax.rem(line, side_x)
    origin = origin + side_x * jnp.where(past < 0, side, far_side)
    table = got_table[...].reshape(count, LANES)
    listed = cross(table.astype(jnp.bfloat16), ones(iota((count, count * slots), 0) == origin))
    listed = jnp.where(iota(listed.shape, 0) == rank, listed, 0.0)
    listed = jnp.sum(listed, axis=0, keepdims=True)
    select = ones(iota((rows, count * slots), 0).astype(jnp.float32) + 1.0 == listed)

    def gather(array, window):
        def lines(ref, number):
            values = ref[array, :, :, window]
            return values.reshape(peers * number, values.shape[-1])

        values = [lines(got_near, slots), lines(got_far, direct)]
        if spill:
            values.append(lines(got_relay, spill))
        high, low = halves(jnp.concatenate(values, axis=0))
        return dot(select, high) + dot(select, low)

    settle_flat(got_near, near_sem, 0)
    if spill:
        settle_flat(got_relay, relay_sem, 0)
    first = []
    for piece, window in enumerate(windows):
        left, size = cuts[piece]
        settle_piece(0, piece)
        pad_a[HALF : HALF + rows, LANES + left : LANES + left + size] = gather(0, window)
        first += exchange(pad_a, piece, left, size)
    for piece in range(AHEAD):
        supply_rise(send_near, got_near, near_sem, 1, piece)
        supply_far(1, piece)
    if spill:
        relay(1)
        supply_flat(send_relay, got_relay, relay_sem, 1)
        for piece in range(AHEAD):
            supply_rise(send_relay, got_relay, relay_sem, 1, piece)
    for piece in range(AHEAD, PIECES):
        supply_rise(send_near, got_near, near_sem, 1, piece)
        if spill:
            supply_rise(send_relay, got_relay, relay_sem, 1, piece)
        supply_far(1, piece)
    for load in loads[4:]:
        load.wait()
    receive(first)
    u_ref[...] = smooth(pad_a)

    second = []
    settle_flat(got_near, near_sem, 1)
    if spill:
        settle_flat(got_relay, relay_sem, 1)
    for piece, window in enumerate(windows):
        left, size = cuts[piece]
        inner = slice(LANES + left, LANES + left + size)
        settle_piece(1, piece)
        root = jnp.sqrt(prior_ref[:, window] + gather(1, window))
        root_ref[:, window] = root
        r0_ref[:, window] = pad_a[HALF : HALF + rows, inner] / root
        u = root * u_ref[:, window]
        u_ref[:, window] = u
        pad_b[HALF : HALF + rows, inner] = root * u
        second += exchange(pad_b, PIECES + piece, left, size)
    r0, u = r0_ref[...], u_ref[...]
    rr, ru = total(r0 * r0), total(r0 * u)
    own = jnp.where(rr > 0.0, ru / rr, 0.0)
    receive(second)
    z = root_ref[...] * smooth(pad_b)
    z_ref[...] = z
    q = own * r0 - u
    g = own * u - z
    lane = iota((1, LANES), 1)
    packed = jnp.zeros((1, LANES), jnp.float32)
    for index, value in enumerate((rr, ru, total(q * q), total(q * g), total(r0 * g))):
        packed = jnp.where(lane == index, value, packed)
    part[...] = packed
    parts[pl.ds(me, 1), 0, :] = packed
    share(lambda other: part, parts, part_sem)
    arrived(parts, part_sem, 0, count - 1)

    table = parts[...].reshape(count, LANES)
    rr_d, ru_d, qq_d, qg_d, rg_d = [table[:, i : i + 1] for i in range(5)]
    rr, ru = total(rr_d), total(ru_d)
    mu = ru / rr
    shift = mu - jnp.where(rr_d > 0.0, ru_d / rr_d, 0.0)
    qq = total(qq_d + shift * shift * rr_d)
    qg = total(qg_d + shift * (rg_d - qq_d) + shift * shift * ru_d)
    alpha0 = rr / (0.5 * rr + ru)
    norm = alpha0 * alpha0 * qq
    beta = norm / rr
    alpha1 = norm / (alpha0 * alpha0 * (0.5 * qq + qg) - beta * norm / alpha0)
    most = jnp.zeros((1, 1), jnp.float32)
    if spill:
        most = jnp.max(got_table[...].reshape(count, LANES), axis=0, keepdims=True)[:, LANES - 1 :]
    flag = jnp.where(most > room, 1.0, 0.0)
    packed = jnp.zeros((1, LANES), jnp.float32)
    for index, value in enumerate((alpha0, alpha1, beta, mu, flag)):
        packed = jnp.where(lane == index, value, packed)
    scalars_ref[...] = packed

    finish(first)
    finish(second)
    arrived(send_table, table_sem, 0, count - 1, way=0)
    for array in range(2):
        settle_flat(send_near, near_sem, array, way=0)
        for piece in range(PIECES):
            settle_rise(send_near, near_sem, array, piece, way=0)
            settle_far(send_far, array, piece, way=0)
        if spill:
            drain(send_spill.at[array], spill_sem, 0, array)
            settle_flat(send_relay, relay_sem, array, way=0)
            for piece in range(PIECES):
                settle_rise(send_relay, relay_sem, array, piece, way=0)
    if spill:
        drain(send_list, spill_sem, 0, 2)
    arrived(parts, part_sem, 0, count - 1, way=0)


def close_kernel(r0_ref, u_ref, z_ref, scalars_ref, field_ref, residual_ref):
    alpha0, alpha1, beta, mu = [scalars_ref[0:1, i : i + 1] for i in range(4)]
    r0, u = r0_ref[...], u_ref[...]
    q = mu * r0 - u
    r1 = alpha0 * q
    field_ref[...] = alpha0 * r0 + alpha1 * (r1 + beta * r0)
    along = alpha0 * (0.5 * q + mu * u - z_ref[...]) + beta * (0.5 * r0 + u)
    residual_ref[...] = r1 - alpha1 * along


def solve(slots, direct, room, identity, arrays):
    ny, nx = lax.axis_size("ty"), lax.axis_size("tx")
    block_tile, block_row, block_sums, block_weights, prior_weight, *matrices = arrays
    count = ny * nx
    blocks, groups, _ = block_sums.shape
    rows, cols = prior_weight.shape
    peers = count // 2
    spill = max(slots - direct, 1)
    vmem = pl.BlockSpec(memory_space=pltpu.VMEM)
    hbm = pl.BlockSpec(memory_space=pltpu.HBM)
    shape = jax.ShapeDtypeStruct((rows, cols), jnp.float32)

    def scratch(*shape):
        return pltpu.VMEM(shape, jnp.float32)

    def semaphores(*shape):
        return pltpu.SemaphoreType.DMA(shape)

    def twice(*shape):
        return [scratch(*shape), scratch(*shape)]

    return pl.pallas_call(
        functools.partial(solve_kernel, ny, nx, slots, direct, room),
        out_shape=(shape, shape, shape, jax.ShapeDtypeStruct((1, LANES), jnp.float32)),
        in_specs=[hbm] * 8,
        out_specs=(vmem,) * 4,
        scratch_shapes=[
            pltpu.VMEM((1, blocks), jnp.int32),
            pltpu.VMEM((1, blocks), jnp.int32),
            *twice(blocks, groups, LANES),
            scratch(rows, cols),
            *[pltpu.VMEM(matrix.shape, matrix.dtype) for matrix in matrices],
            scratch(rows, cols),
            semaphores(8),
            *twice(count, 1, LANES),
            *twice(2, peers, slots, cols),
            *twice(2, peers, direct, cols),
            *twice(2, max(room, 8), cols),
            *twice(2, peers, spill, cols),
            *twice(1, LANES),
            *twice(rows + 2 * HALF, cols + 2 * LANES),
            scratch(1, LANES),
            scratch(count, 1, LANES),
            semaphores(2, 1),
            semaphores(2, 2 + 2 * PIECES),
            semaphores(2, 2 * PIECES),
            semaphores(2, 3),
            semaphores(2, 2 + 2 * PIECES),
            semaphores(2 * PIECES, 8),
            semaphores(2 * PIECES, 8),
            semaphores(2, 1),
        ],
        compiler_params=pltpu.CompilerParams(
            collective_id=identity, has_side_effects=True, vmem_limit_bytes=LIMIT
        ),
    )(*[pltpu.with_memory_space_constraint(array, pltpu.HBM) for array in arrays])


def close(r0, u, z, scalars):
    vmem = pl.BlockSpec(memory_space=pltpu.VMEM)
    shape = jax.ShapeDtypeStruct(r0.shape, jnp.float32)
    return pl.pallas_call(
        close_kernel, out_shape=(shape, shape), in_specs=[vmem] * 4, out_specs=(vmem, vmem),
        compiler_params=pltpu.CompilerParams(vmem_limit_bytes=LIMIT),
    )(r0, u, z, scalars)


def shards(block_sums, block_weights, block_tile, block_row, prior_weight):
    count = lax.axis_size("ty") * lax.axis_size("tx")
    blocks, band, cols = block_sums.shape
    slots = 2 * blocks // count
    arrays = (
        block_tile.reshape(1, blocks),
        block_row.reshape(1, blocks),
        block_sums.reshape(blocks * band, cols // LANES, LANES),
        block_weights.reshape(blocks * band, cols // LANES, LANES),
        prior_weight,
        *kernel_matrices(prior_weight.shape[0], 2 * LANES),
    )
    fields = solve(slots, slots // 2, blocks // 4, 0, arrays)
    return lax.cond(
        fields[3][0, 4] > 0.5,
        lambda fields: close(*solve(slots, slots, 0, 1, arrays)),
        lambda fields: close(*fields),
        fields,
    )


def solution(mesh):
    in_specs = (
        P(("ty", "tx"), None, None),
        P(("ty", "tx"), None, None),
        P(("ty", "tx"), None),
        P(("ty", "tx")),
        P("ty", "tx"),
    )
    out_specs = (P("ty", "tx"), P("ty", "tx"))
    return jax.shard_map(shards, mesh=mesh, in_specs=in_specs, out_specs=out_specs, check_vma=False)
```
